32 devices in a mesh: region: 16 (over z, y, x), tm: 2 (over core).
Axes of the slice: x: 2, y: 2, z: 4, core: 2. Of those that a mesh axis runs over, the one named last changes fastest.
Arguments:
- latents: bfloat16 [16, 256, 768], P('region', 'tm')
- output_grad: bfloat16 [16, 256, 768], P('region', 'tm'), may hold values from -6 to 6
- conv_kernel: float32 [4, 768], replicated, may hold values from -1 to 1
- w_query: bfloat16 [768, 768], replicated, may hold values from -0.21875 to 0.21875
- w_key: bfloat16 [768, 768], replicated, may hold values from -0.21875 to 0.21875
- w_value: bfloat16 [768, 768], replicated, may hold values from -0.21875 to 0.21875
- w_out: bfloat16 [768, 768], replicated, may hold values from -0.21875 to 0.21875
- live_counts: int32 [16, 2], P('region', 'tm'), may hold values from 1 to 128, as said below
Outputs:
- input_grad: bfloat16 [16, 256, 768], P('region', 'tm')
The draws below stay inside these ranges and needn't reach their ends.
Inputs may be any that keep to these rules, and one draw needn't show every extreme that they name: The first live_counts[r, c] of the 128 tokens of region r in span c are valid.
All inputs are finite; a program needn't handle non-finite values.
Results may differ from the reference program's by a relative error of at most 0.018.
The reference program's roundings to bfloat16 on the way (of `hidden`, `grad_proj`, `score_grad` and `query_grad`) count: a program that leaves them out, or rounds other values in their place, can miss the bound.
Values may be sent and summed in bfloat16 or wider, within the bound.
A program may use at most 128 MiB of HBM per device.

```python
import math
import jax
import jax.numpy as jnp
from jax import lax

D = 768
H = 12
HD = 64
KW = 4
TCH = 128
REGIONS = 16
TIME = 256
N_REGION = 16
N_TM = 2


def draw_latents(key, part):
    base = jax.random.normal(key, (REGIONS, TIME, D), jnp.float32)
    return base.astype(jnp.bfloat16)


def draw_live_counts(key, part):
    first = jax.random.randint(jax.random.fold_in(key, 11), (REGIONS, N_TM), 1, TCH + 1)
    second = jax.random.randint(jax.random.fold_in(key, 12), (REGIONS, N_TM), 1, TCH + 1)
    counts = jnp.minimum(first, second)
    counts = counts.at[0].set(TCH)
    return counts.astype(jnp.int32)


def steps_of(stream_key, dims, cuts, least, high):
    gain = 1.0
    for dim, shards_of in cuts:
        steps = jax.random.uniform(jax.random.fold_in(jax.random.fold_in(stream_key, 6), dim), (shards_of,), jnp.float32, least / len(cuts), high / len(cuts))
        gain = gain * jnp.repeat(jnp.exp(steps), dims[dim] // shards_of).reshape((-1,) + (1,) * (len(dims) - 1 - dim))
    return gain


def scatter_about(key, extent, spread, bound, pieces=(), kind=jnp.bfloat16):
    values = spread * jax.random.normal(key, extent, jnp.float32)
    if pieces:
        values = values * steps_of(key, extent, pieces, -0.22, 0.18)
    return jnp.clip(values, -bound, bound).astype(kind)


def setup_inputs(seed: int = 0) -> dict:
    splits = jax.random.split(jax.random.key(seed), 9)
    return {
        "latents": draw_latents(jax.random.fold_in(splits[8], 71), 0),
        "output_grad": scatter_about(splits[1], (REGIONS, TIME, D), 1.0, 6.0, ((0, 16), (1, 2))),
        "conv_kernel": jnp.clip(jax.random.uniform(splits[2], (KW, D), jnp.float32, -1.0, 1.0), -1.0, 1.0),
        "w_query": scatter_about(splits[3], (D, D), D ** -0.5, 0.21875),
        "w_key": scatter_about(splits[4], (D, D), D ** -0.5, 0.21875),
        "w_value": scatter_about(splits[5], (D, D), D ** -0.5, 0.21875),
        "w_out": scatter_about(splits[6], (D, D), D ** -0.5, 0.21875),
        "live_counts": draw_live_counts(jax.random.fold_in(splits[8], 71), 0),
    }


def rounded(values_in):
    return lax.optimization_barrier(values_in.astype(jnp.bfloat16)).astype(jnp.float32)

def causal_conv(signal, kernel):
    length = signal.shape[1]
    padded = jnp.pad(signal, ((0, 0), (KW - 1, 0), (0, 0)))
    result = jnp.zeros_like(signal)
    for offset in range(KW):
        result = result + kernel[offset] * padded[:, KW - 1 - offset:KW - 1 - offset + length, :]
    return result

def conv_transpose(grads, kernel):
    length = grads.shape[1]
    padded = jnp.pad(grads, ((0, 0), (0, KW - 1), (0, 0)))
    result = jnp.zeros_like(grads)
    for offset in range(KW):
        result = result + kernel[offset] * padded[:, offset:offset + length, :]
    return result

def head_grads(operands):
    query_rows, key_rows, value_rows, grad_rows, key_mask = operands
    inv_root = 1.0 / math.sqrt(HD)
    logits = jnp.where(key_mask[None, :], jnp.dot(query_rows, key_rows.T) * inv_root, -1e+30)
    top_logit = lax.optimization_barrier(jnp.max(logits, axis=1, keepdims=True))
    log_total = top_logit + jnp.log(lax.optimization_barrier(jnp.sum(jnp.exp(logits - top_logit), axis=1, keepdims=True)))
    attention = jnp.exp(logits - log_total)
    weight_grad = jnp.dot(grad_rows, value_rows.T)
    row_delta = lax.optimization_barrier(jnp.sum(attention * weight_grad, axis=1, keepdims=True))
    score_grad = rounded(attention * (weight_grad - row_delta))
    query_grad = jnp.dot(score_grad, key_rows) * inv_root
    groups = N_REGION
    per_group = query_rows.shape[0] // groups
    key_count = key_rows.shape[0]
    key_part = jnp.einsum('gqk,gqd->gkd', score_grad.reshape(groups, per_group, key_count), query_rows.reshape(groups, per_group, HD)) * inv_root
    value_part = jnp.einsum('gqk,gqd->gkd', rounded(attention).reshape(groups, per_group, key_count), grad_rows.reshape(groups, per_group, HD))
    key_sum = rounded(lax.optimization_barrier(jnp.sum(rounded(key_part), axis=0)))
    value_sum = rounded(lax.optimization_barrier(jnp.sum(rounded(value_part), axis=0)))
    return (query_grad, key_sum, value_sum)

def make_span_grads(w_key, w_value):

    def span_grads(operands):
        query_rows, key_rows, value_rows, grad_rows, key_mask = operands

        def heads_first(array_in):
            return array_in.astype(jnp.float32).reshape(-1, H, HD).transpose(1, 0, 2)
        head_masks = jnp.broadcast_to(key_mask, (H, key_mask.shape[0]))
        query_part, key_sum, value_sum = lax.map(head_grads, (heads_first(query_rows), heads_first(key_rows), heads_first(value_rows), heads_first(grad_rows), head_masks))

        def flat_rows(array_in):
            return array_in.transpose(1, 0, 2).reshape(-1, H * HD).astype(jnp.bfloat16)
        side_grad = jnp.dot(flat_rows(key_sum), w_key.T, preferred_element_type=jnp.float32)
        side_grad = side_grad + jnp.dot(flat_rows(value_sum), w_value.T, preferred_element_type=jnp.float32)
        return (query_part.transpose(1, 0, 2).reshape(-1, H * HD), side_grad)
    return span_grads

def reference(latents, output_grad, conv_kernel, w_query, w_key, w_value, w_out, live_counts):
    regions, total_time, model_width = latents.shape
    hidden = causal_conv(latents.astype(jnp.float32), conv_kernel).astype(jnp.bfloat16)
    flattened = hidden.reshape(-1, model_width)
    queries = jnp.dot(flattened, w_query, preferred_element_type=jnp.float32).astype(jnp.bfloat16)
    key_proj = jnp.dot(flattened, w_key, preferred_element_type=jnp.float32).astype(jnp.bfloat16)
    value_proj = jnp.dot(flattened, w_value, preferred_element_type=jnp.float32).astype(jnp.bfloat16)
    position = lax.broadcasted_iota(jnp.int32, (regions, N_TM, TCH), 2)
    valid = position < live_counts[:, :, None]
    query_live = valid.reshape(regions * total_time, 1).astype(jnp.float32)
    grad_proj = (jnp.dot(output_grad.reshape(-1, model_width), w_out.T, preferred_element_type=jnp.float32) * query_live).astype(jnp.bfloat16)

    def by_span(array_in):
        return array_in.reshape(regions, N_TM, TCH, model_width).transpose(1, 0, 2, 3).reshape(N_TM, regions * TCH, model_width)
    key_mask = valid.transpose(1, 0, 2).reshape(N_TM, regions * TCH)
    query_part, side_part = lax.map(make_span_grads(w_key, w_value), (by_span(queries), by_span(key_proj), by_span(value_proj), by_span(grad_proj), key_mask))

    def by_region(array_in):
        return array_in.reshape(N_TM, regions, TCH, model_width).transpose(1, 0, 2, 3).reshape(-1, model_width)
    query_grad = by_region(query_part).astype(jnp.bfloat16)
    side_grad = by_region(side_part)
    hidden_grad = jnp.dot(query_grad, w_query.T, preferred_element_type=jnp.float32) + side_grad
    input_grad = conv_transpose(hidden_grad.reshape(regions, total_time, model_width), conv_kernel)
    return input_grad.astype(jnp.bfloat16)
```

```python
import functools
import math

import jax
import jax.numpy as jnp
from jax import lax
from jax.experimental import pallas as pl
from jax.experimental.pallas import tpu as pltpu
from jax.sharding import PartitionSpec as P

H = 12
KW = 4
BLK = 256
PAGE = 16
CAPS = (1024, 1280)
NEG = -1e30
bf16 = jnp.bfloat16
f32 = jnp.float32
i32 = jnp.int32
VM = pl.BlockSpec(memory_space=pltpu.VMEM)
SM = pl.BlockSpec(memory_space=pltpu.SMEM)
ANY = pl.BlockSpec(memory_space=pl.ANY)
MESH = pl.DeviceIdType.MESH


def dot(a, b):
    return jnp.dot(a, b, preferred_element_type=f32)


def dot_t(a, b):
    return lax.dot_general(a, b, (((1,), (1,)), ((), ())), preferred_element_type=f32)


def owner(h, n_reg):
    return (h * n_reg) // H


def head_of(me, n_reg):
    h = (me * H + n_reg - 1) // n_reg
    return jnp.minimum(h, H - 1), jnp.logical_and(h < H, owner(h, n_reg) == me)


def peer(me, step, n):
    if n & (n - 1):
        return lax.rem(me + step, n)
    out = me
    for b in range(n.bit_length() - 1):
        if step >> b & 1:
            w = 1 << b
            out = out + w * (1 - 2 * ((me // w) % 2))
    return out


def caps_of(n):
    return [c for c in CAPS if c < n] + [-(-n // 1024) * 1024]


def spread_kernel(
    n_reg, n_tm, caps, lat_ref, og_ref, ck_ref, cnt_ref, wq_ref, wk_ref, wv_ref, wo_ref,
    out_ref, table_ref, pick_ref,
    wbuf, lat, og, ext, edge, send, csend, cbuf, wsem, esem, ssem, rsem, tsem, lsem,
):
    me = lax.axis_index("region")
    mt = lax.axis_index("tm")
    t, d = lat_ref.shape[1], lat_ref.shape[2]
    hd = d // H
    barrier = pltpu.get_barrier_semaphore()
    others = [
        (k, c) for k in reversed(range(n_reg)) for c in range(n_tm) if (k, c) != (0, 0)
    ]

    def place(k, c):
        return {"region": peer(me, k, n_reg), "tm": lax.rem(mt + c, n_tm)}

    for k, c in others:
        pl.semaphore_signal(barrier, inc=1, device_id=place(k, c), device_id_type=MESH)
    loads = [
        pltpu.make_async_copy(ref, dst, wsem.at[i])
        for i, (ref, dst) in enumerate(
            (
                (lat_ref.at[0], lat),
                (og_ref.at[0], og),
                (wo_ref, wbuf.at[0]),
                (wv_ref, wbuf.at[1]),
                (wq_ref, wbuf.at[2]),
                (wk_ref, wbuf.at[3]),
            )
        )
    ]
    for load in loads:
        load.start()
    head, is_head = head_of(me, n_reg)

    count = cnt_ref[0, 0]
    csend[...] = jnp.zeros(csend.shape, i32) + count
    cbuf[mt, me] = jnp.zeros(csend.shape, i32) + count

    def hide(rows):
        hidden = ck_ref[0:1, :] * ext[8 : 8 + rows, :]
        for j in range(1, KW):
            hidden = hidden + ck_ref[j : j + 1, :] * ext[8 - j : 8 - j + rows, :]
        return hidden.astype(bf16)

    def put(x, rows, half, first):
        for h in range(H):
            part = x[:, h * hd : (h + 1) * hd].reshape(rows // PAGE, PAGE, hd)
            send[h, half, 0 : rows // PAGE, :, first : first + hd] = part

    loads[0].wait()
    ext[0:8, :] = jnp.zeros((8, d), f32)
    ext[8 : 8 + t, :] = lat[...].astype(f32)
    hidden = hide(t)
    loads[1].wait()
    loads[2].wait()
    live = lax.broadcasted_iota(i32, (t, 1), 0) < count
    g = jnp.where(live, dot_t(og[...], wbuf[0]), 0.0).astype(bf16)
    put(g, t, 1, hd)
    loads[3].wait()
    put(dot(hidden, wbuf[1]).astype(bf16), t, 1, 0)

    pl.semaphore_wait(barrier, len(others))
    to_next = pltpu.make_async_remote_copy(
        src_ref=lat.at[pl.ds(t - 16, 16)],
        dst_ref=edge,
        send_sem=esem.at[0],
        recv_sem=esem.at[1],
        device_id={"tm": jnp.minimum(mt + 1, n_tm - 1)},
        device_id_type=MESH,
    )

    @pl.when(mt < n_tm - 1)
    def _():
        to_next.start()

    parts = (
        (1, pl.ds(1, t // PAGE - 1)),
        (0, pl.ds(1, t // PAGE - 1)),
        (slice(None), pl.ds(0, 1)),
    )

    def away(k, i):
        target = peer(me, k, n_reg)
        half, rows = parts[i]
        return pltpu.make_async_remote_copy(
            src_ref=send.at[head_of(target, n_reg)[0], half, rows],
            dst_ref=out_ref.at[half, me, rows],
            send_sem=ssem.at[i, k],
            recv_sem=rsem.at[i, me],
            device_id={"region": target},
            device_id_type=MESH,
        )

    def each(act):
        for k in reversed(range(1, n_reg)):

            @pl.when(head_of(peer(me, k, n_reg), n_reg)[1])
            def _():
                act(k)

    def tell(j):
        return pltpu.make_async_remote_copy(
            src_ref=csend,
            dst_ref=cbuf.at[mt, me],
            send_sem=tsem.at[0, j],
            recv_sem=tsem.at[1, mt * n_reg + me],
            device_id=place(*others[j]),
            device_id_type=MESH,
        )

    each(lambda k: away(k, 0).start())
    for j in range(len(others)):
        tell(j).start()
    loads[4].wait()
    put(dot(hidden, wbuf[2]).astype(bf16), t, 0, 0)
    loads[5].wait()
    put(dot(hidden, wbuf[3]).astype(bf16), t, 0, hd)
    each(lambda k: away(k, 1).start())

    @pl.when(mt > 0)
    def _():
        to_next.wait_recv()
        ext[0:8, :] = edge[8:16, :].astype(f32)
        top = hide(16)
        put(dot(top, wbuf[1]).astype(bf16), 16, 1, 0)
        put(dot(top, wbuf[2]).astype(bf16), 16, 0, 0)
        put(dot(top, wbuf[3]).astype(bf16), 16, 0, hd)

    each(lambda k: away(k, 2).start())
    here = pltpu.make_async_copy(send.at[head], out_ref.at[:, me], lsem.at[0])

    @pl.when(is_head)
    def _():
        here.start()

    for j in range(len(others)):
        k, c = others[j]
        where = place(k, c)
        slot = where["tm"] * n_reg + where["region"]
        pltpu.make_async_copy(csend, cbuf.at[where["tm"], where["region"]], tsem.at[1, slot]).wait()
    pages = t // PAGE
    zero = jnp.zeros(csend.shape, i32)
    slot = lax.broadcasted_iota(i32, csend.shape, 1)

    def used(c, r):
        return (cbuf[c, r] + (PAGE - 1)) // PAGE

    most = zero
    for c in range(n_tm):
        total = zero
        for r in range(n_reg):
            total = total + used(c, r)
        most = jnp.maximum(most, total)
    pick = zero
    for cap in caps[:-1]:
        pick = pick + jnp.where(most * PAGE > cap, 1, 0)
    pick_ref[0, 0] = jnp.max(pick.astype(f32)).astype(i32)
    end, source, rows_left, begin = zero, zero, zero, zero
    for r in range(n_reg):
        n = used(mt, r)
        mine = jnp.logical_and(slot >= end, slot < end + n)
        source = jnp.where(mine, slot - end + r * pages, source)
        rows_left = jnp.where(mine, cbuf[mt, r] - (slot - end) * PAGE, rows_left)
        begin = jnp.where(slot == r, end, begin)
        end = end + n
    counts = zero
    for r in range(n_reg):
        counts = jnp.where(slot == r, cbuf[mt, r], counts)
    for i, row in enumerate((source, rows_left, begin, counts)):
        table_ref[i : i + 1, :] = row

    def done(k):
        for i in range(3):
            away(k, i).wait_send()

    each(done)
    for j in range(len(others)):
        tell(j).wait_send()

    @pl.when(mt < n_tm - 1)
    def _():
        to_next.wait_send()

    @pl.when(is_head)
    def _():
        here.wait()
        for k in range(1, n_reg):
            s = peer(me, k, n_reg)
            for i, (half, rows) in enumerate(parts):
                there = out_ref.at[half, s, rows]
                pltpu.make_async_copy(send.at[0, half, rows], there, rsem.at[i, s]).wait()


def work_kernel(
    n_reg, n_tm, cap, chunk_ref, tbl_ref, ck_ref, wq_ref, wk_ref, wv_ref,
    out_ref,
    chunk, qk, ka, vg, kt, qt, gt, qg, sbuf, wbuf, dkv, dqp, part,
    got, wts, xs, ext, wsem, esem, ssem, rsem, lsem,
):
    me = lax.axis_index("region")
    mt = lax.axis_index("tm")
    t, d = out_ref.shape[1], out_ref.shape[2]
    hd = d // H
    width = 2 * hd
    inv_root = 1.0 / math.sqrt(hd)
    blocks = cap // BLK
    subs = blocks if blocks <= 5 else 4
    supers = blocks // subs
    step = BLK // PAGE
    barrier = pltpu.get_barrier_semaphore()
    head, is_head = head_of(me, n_reg)

    def each(act):
        for k in reversed(range(1, n_reg)):
            r = peer(me, k, n_reg)

            @pl.when(head_of(r, n_reg)[1])
            def _():
                act(r)

    each(
        lambda r: pl.semaphore_signal(
            barrier, inc=1, device_id={"region": r}, device_id_type=MESH
        )
    )

    @pl.when(mt < n_tm - 1)
    def _():
        up = {"tm": jnp.minimum(mt + 1, n_tm - 1)}
        pl.semaphore_signal(barrier, inc=1, device_id=up, device_id_type=MESH)

    fetch = pltpu.make_async_copy(chunk_ref, chunk, lsem.at[1])

    @pl.when(is_head)
    def _():
        fetch.start()

    loads = [
        pltpu.make_async_copy(ref, wts.at[i], wsem.at[i])
        for i, ref in enumerate((wq_ref, wk_ref, wv_ref))
    ]
    for load in loads:
        load.start()
    peers = jnp.where(is_head, n_reg - 1, 0) + jnp.minimum(mt, 1)

    def lane(rows):
        return lax.broadcasted_iota(i32, (rows, width), 1)

    def away(r, k):
        return pltpu.make_async_remote_copy(
            src_ref=part.at[r],
            dst_ref=got.at[head],
            send_sem=ssem.at[k],
            recv_sem=rsem.at[head],
            device_id={"region": r},
            device_id_type=MESH,
        )

    here = pltpu.make_async_copy(part.at[me], got.at[head], lsem.at[0])

    @pl.when(is_head)
    def _():
        fetch.wait()

        def pack(p, c):
            source = tbl_ref[0, p]
            rows = tbl_ref[1, p]
            a = chunk[0, source]
            b = chunk[1, source]
            dead = lax.broadcasted_iota(i32, (PAGE, width), 0) >= rows
            bias = jnp.where(jnp.logical_and(lane(PAGE) == 0, dead), NEG, 0.0)
            to = pl.ds(pl.multiple_of(p * PAGE, PAGE), PAGE)
            qk[to, :] = a
            ka[to, :] = jnp.where(lane(PAGE) < hd, bias, a.astype(f32)).astype(bf16)
            vg[to, :] = jnp.where(dead, 0.0, b.astype(f32)).astype(bf16)
            return c

        lax.fori_loop(0, cap // PAGE, pack, 0, unroll=4)

        def ready(i, c):
            at = pl.multiple_of(i * BLK, BLK)
            a = qk[pl.ds(at, BLK), :]
            b = vg[pl.ds(at, BLK), :]
            a_t = a.T
            scaled = (a_t[0:hd, :].astype(f32) * inv_root).astype(bf16)
            one = jnp.where(lax.broadcasted_iota(i32, (hd, BLK), 0) == 0, 1.0, 0.0)
            qt[i] = jnp.concatenate([one.astype(bf16), scaled], axis=0)
            kt[i] = a_t[hd:, :]
            gt[i] = jnp.concatenate([b.T[hd:, :], jnp.zeros((hd, BLK), bf16)], axis=0)
            low = lane(BLK) < hd
            qg[i, 0:BLK, :] = jnp.where(low, a.astype(f32) * inv_root, 0.0).astype(bf16)
            qg[i, BLK:, :] = jnp.where(low, 0.0, b.astype(f32)).astype(bf16)
            dkv[pl.ds(i * step, step)] = jnp.zeros((step, PAGE, width), f32)
            return c

        lax.fori_loop(0, blocks, ready, 0)

        def fold(x, op):
            return op(x.reshape(BLK // 8, 8, BLK), axis=0)

        def per_queries(qi, c):
            qat, gat = qt[qi], gt[qi]

            def first(ki, m):
                for u in range(subs):
                    kat = pl.multiple_of((ki * subs + u) * BLK, BLK)
                    s = dot(ka[pl.ds(kat, BLK), :], qat)
                    wbuf[ki * subs + u] = dot(vg[pl.ds(kat, BLK), :], gat)
                    sbuf[ki * subs + u] = s
                    m = jnp.maximum(m, fold(s, jnp.max))
                return m

            m = lax.fori_loop(0, supers, first, jnp.full((8, BLK), NEG, f32))
            m = jnp.max(m, axis=0, keepdims=True)

            def middle(ki, carry):
                l, dl = carry
                for u in range(subs):
                    p = jnp.exp(sbuf[ki * subs + u] - m)
                    sbuf[ki * subs + u] = p
                    l = l + fold(p, jnp.sum)
                    dl = dl + fold(p * wbuf[ki * subs + u], jnp.sum)
                return l, dl

            none = jnp.zeros((8, BLK), f32)
            l, dl = lax.fori_loop(0, supers, middle, (none, none))
            inv_l = 1.0 / jnp.sum(l, axis=0, keepdims=True)
            delta = jnp.sum(dl, axis=0, keepdims=True) * inv_l
            both = qg[qi]

            def last(ki, dq):
                for u in range(subs):
                    att = sbuf[ki * subs + u] * inv_l
                    ds = (att * (wbuf[ki * subs + u] - delta)).astype(bf16)
                    pair = jnp.concatenate([ds, att.astype(bf16)], axis=1)
                    to = pl.ds((ki * subs + u) * step, step)
                    dkv[to] += dot(pair, both).reshape(step, PAGE, width)
                    dq = dq + dot(kt[ki * subs + u], ds)
                return dq

            dq = lax.fori_loop(0, supers, last, jnp.zeros((hd, BLK), f32))
            dq = jnp.concatenate([dq * inv_root, jnp.zeros((hd, BLK), f32)], axis=0)
            dqp[pl.ds(qi * step, step)] = dq.T.reshape(step, PAGE, width)
            return c

        lax.fori_loop(0, blocks, per_queries, 0)

    @pl.when(peers > 0)
    def _():
        pl.semaphore_wait(barrier, peers)

    @pl.when(is_head)
    def _():
        for k in reversed(range(n_reg)):
            r = peer(me, k, n_reg)
            begin = tbl_ref[2, r]
            live = lax.broadcasted_iota(i32, (t, width), 0) < tbl_ref[3, r]

            def rows_of(ref):
                pages = [ref[begin + j] for j in range(t // PAGE)]
                return jnp.where(live, jnp.concatenate(pages, axis=0), 0.0)

            both, dq = rows_of(dkv), rows_of(dqp)
            part[r, 0:t, :] = both.astype(bf16)
            pair = jnp.concatenate([dq[0 : t // 2, 0:hd], dq[t // 2 :, 0:hd]], axis=1)
            part[r, t:, :] = pair.astype(bf16)
            if k:
                away(r, k).start()
            else:
                here.start()
        here.wait()

    for h in range(H):

        @pl.when(owner(h, n_reg) != me)
        def _():
            pltpu.make_async_copy(part.at[0], got.at[h], rsem.at[h]).wait()

    for h in range(H):
        cols = slice(h * hd, (h + 1) * hd)
        xs[0, 0 : t // 2, cols] = got[h, t:, 0:hd]
        xs[0, t // 2 :, cols] = got[h, t:, hd:]
        xs[1, :, cols] = got[h, 0:t, 0:hd]
        xs[2, :, cols] = got[h, 0:t, hd:]
    for load in loads:
        load.wait()
    side = dot_t(xs[1], wts[1]) + dot_t(xs[2], wts[2])
    ext[0:t, :] = dot_t(xs[0], wts[0]) + side

    to_prev = pltpu.make_async_remote_copy(
        src_ref=ext.at[pl.ds(0, 8)],
        dst_ref=ext.at[pl.ds(t, 8)],
        send_sem=esem.at[0],
        recv_sem=esem.at[1],
        device_id={"tm": jnp.maximum(mt - 1, 0)},
        device_id_type=MESH,
    )

    @pl.when(mt > 0)
    def _():
        to_prev.start()

    @pl.when(is_head)
    def _():
        for k in range(1, n_reg):
            away(peer(me, k, n_reg), k).wait_send()

    @pl.when(mt == n_tm - 1)
    def _():
        ext[t : t + 8, :] = jnp.zeros((8, d), f32)

    @pl.when(mt < n_tm - 1)
    def _():
        to_prev.wait_recv()

    total = ck_ref[0:1, :] * ext[0:t, :]
    for j in range(1, KW):
        total = total + ck_ref[j : j + 1, :] * ext[j : j + t, :]
    out_ref[0] = total.astype(bf16)

    @pl.when(mt > 0)
    def _():
        to_prev.wait_send()


def shards(n_reg, n_tm, latents, output_grad, conv_kernel, w_query, w_key, w_value, w_out, live_counts):
    _, t, d = latents.shape
    hd = d // H
    dma = pltpu.SemaphoreType.DMA
    caps = caps_of(n_reg * t)
    lanes = max(128, n_reg * t // PAGE)
    chunks, table, pick = pl.pallas_call(
        functools.partial(spread_kernel, n_reg, n_tm, caps),
        out_shape=(
            jax.ShapeDtypeStruct((2, n_reg, t // PAGE, PAGE, 2 * hd), bf16),
            jax.ShapeDtypeStruct((4, lanes), i32),
            jax.ShapeDtypeStruct((1, 1), i32),
        ),
        in_specs=[ANY, ANY, VM, SM, ANY, ANY, ANY, ANY],
        out_specs=(ANY, VM, SM),
        scratch_shapes=[
            pltpu.VMEM((4, d, d), bf16),
            pltpu.VMEM((t, d), bf16),
            pltpu.VMEM((t, d), bf16),
            pltpu.VMEM((t + 8, d), f32),
            pltpu.VMEM((16, d), bf16),
            pltpu.VMEM((H, 2, t // PAGE, PAGE, 2 * hd), bf16),
            pltpu.VMEM((1, lanes), i32),
            pltpu.VMEM((n_tm, n_reg, 1, lanes), i32),
            dma((6,)),
            dma((2,)),
            dma((3, n_reg)),
            dma((3, n_reg)),
            dma((2, n_reg * n_tm)),
            dma((1,)),
        ],
        compiler_params=pltpu.CompilerParams(collective_id=0, has_side_effects=True),
        name="spread",
    )(latents, output_grad, conv_kernel, live_counts, w_query, w_key, w_value, w_out)

    def work(i, cap):
        blocks = cap // BLK
        return pl.pallas_call(
            functools.partial(work_kernel, n_reg, n_tm, cap),
            out_shape=jax.ShapeDtypeStruct((1, t, d), bf16),
            in_specs=[ANY, SM, VM, ANY, ANY, ANY],
            out_specs=VM,
            scratch_shapes=[
                pltpu.VMEM((2, n_reg * t // PAGE, PAGE, 2 * hd), bf16),
                pltpu.VMEM((cap, 2 * hd), bf16),
                pltpu.VMEM((cap, 2 * hd), bf16),
                pltpu.VMEM((cap, 2 * hd), bf16),
                pltpu.VMEM((blocks, hd, BLK), bf16),
                pltpu.VMEM((blocks, 2 * hd, BLK), bf16),
                pltpu.VMEM((blocks, 2 * hd, BLK), bf16),
                pltpu.VMEM((blocks, 2 * BLK, 2 * hd), bf16),
                pltpu.VMEM((blocks, BLK, BLK), f32),
                pltpu.VMEM((blocks, BLK, BLK), f32),
                pltpu.VMEM(((cap + t) // PAGE, PAGE, 2 * hd), f32),
                pltpu.VMEM(((cap + t) // PAGE, PAGE, 2 * hd), f32),
                pltpu.VMEM((n_reg, t + t // 2, 2 * hd), bf16),
                pltpu.VMEM((H, t + t // 2, 2 * hd), bf16),
                pltpu.VMEM((3, d, d), bf16),
                pltpu.VMEM((3, t, d), bf16),
                pltpu.VMEM((t + 8, d), f32),
                dma((3,)),
                dma((2,)),
                dma((n_reg,)),
                dma((H,)),
                dma((2,)),
            ],
            compiler_params=pltpu.CompilerParams(collective_id=i + 1, has_side_effects=True),
            name=f"work{cap}",
        )

    return lax.switch(
        pick[0, 0],
        [work(i, cap) for i, cap in enumerate(caps)],
        chunks.reshape(2, n_reg * t // PAGE, PAGE, 2 * hd), table, conv_kernel, w_query, w_key, w_value,
    )


def solution(mesh):
    shard = P("region", "tm", None)
    in_specs = (shard, shard, P(), P(), P(), P(), P(), P("region", "tm"))
    body = functools.partial(shards, mesh.shape["region"], mesh.shape["tm"])
    return jax.shard_map(body, mesh=mesh, in_specs=in_specs, out_specs=shard, check_vma=False)
```

```python
import functools
import math

import jax
import jax.numpy as jnp
from jax import lax
from jax.experimental import pallas as pl
from jax.experimental.pallas import tpu as pltpu
from jax.sharding import PartitionSpec as P

H = 12
KW = 4
BLK = 256
PAGE = 16
CAPS = (1024, 1280)
NEG = -1e30
bf16 = jnp.bfloat16
f32 = jnp.float32
i32 = jnp.int32
VM = pl.BlockSpec(memory_space=pltpu.VMEM)
SM = pl.BlockSpec(memory_space=pltpu.SMEM)
ANY = pl.BlockSpec(memory_space=pl.ANY)
MESH = pl.DeviceIdType.MESH


def dot(a, b):
    return jnp.dot(a, b, preferred_element_type=f32)


def dot_t(a, b):
    return lax.dot_general(a, b, (((1,), (1,)), ((), ())), preferred_element_type=f32)


def owner(h, n_reg, mt):
    base = (h * n_reg) // H
    if n_reg % 4:
        return base
    return base // 4 * 4 + (base + base // 4 + 2 * mt) % 4


def head_of(me, n_reg, mt):
    base = me
    if n_reg % 4 == 0:
        base = me // 4 * 4 + (me + 3 * (me // 4) + 2 * mt) % 4
    h = (base * H + n_reg - 1) // n_reg
    return jnp.minimum(h, H - 1), jnp.logical_and(h < H, (h * n_reg) // H == base)


def peer(me, step, n):
    return lax.rem(me + step, n)


def caps_of(n):
    return [c for c in CAPS if c < n] + [-(-n // 1024) * 1024]


def spread_kernel(
    n_reg, n_tm, caps, lat_ref, og_ref, ck_ref, cnt_ref, wq_ref, wk_ref, wv_ref, wo_ref,
    out_ref, table_ref, pick_ref,
    wbuf, lat, og, ext, edge, send, csend, cbuf, wsem, esem, ssem, rsem, tsem, lsem,
):
    me = lax.axis_index("region")
    mt = lax.axis_index("tm")
    t, d = lat_ref.shape[1], lat_ref.shape[2]
    hd = d // H
    barrier = pltpu.get_barrier_semaphore()
    others = [
        (k, c) for k in range(n_reg) for c in range(n_tm) if (k, c) != (0, 0)
    ]

    def place(k, c):
        return {"region": peer(me, k, n_reg), "tm": lax.rem(mt + c, n_tm)}

    for k, c in others:
        pl.semaphore_signal(barrier, inc=1, device_id=place(k, c), device_id_type=MESH)
    loads = [
        pltpu.make_async_copy(ref, dst, wsem.at[i])
        for i, (ref, dst) in enumerate(
            (
                (lat_ref.at[0], lat),
                (og_ref.at[0], og),
                (wo_ref, wbuf.at[0]),
                (wv_ref, wbuf.at[1]),
                (wq_ref, wbuf.at[2]),
                (wk_ref, wbuf.at[3]),
            )
        )
    ]
    for load in loads:
        load.start()
    head, is_head = head_of(me, n_reg, mt)

    count = cnt_ref[0, 0]
    csend[...] = jnp.zeros(csend.shape, i32) + count
    cbuf[mt, me] = jnp.zeros(csend.shape, i32) + count

    def hide(rows):
        hidden = ck_ref[0:1, :] * ext[8 : 8 + rows, :]
        for j in range(1, KW):
            hidden = hidden + ck_ref[j : j + 1, :] * ext[8 - j : 8 - j + rows, :]
        return hidden.astype(bf16)

    def put(x, rows, half, first):
        for h in range(H):
            part = x[:, h * hd : (h + 1) * hd].reshape(rows // PAGE, PAGE, hd)
            send[h, half, 0 : rows // PAGE, :, first : first + hd] = part

    loads[0].wait()
    ext[0:8, :] = jnp.zeros((8, d), f32)
    ext[8 : 8 + t, :] = lat[...].astype(f32)
    hidden = hide(t)
    loads[1].wait()
    loads[2].wait()
    live = lax.broadcasted_iota(i32, (t, 1), 0) < count
    g = jnp.where(live, dot_t(og[...], wbuf[0]), 0.0).astype(bf16)
    put(g, t, 1, hd)
    loads[3].wait()
    put(dot(hidden, wbuf[1]).astype(bf16), t, 1, 0)

    pl.semaphore_wait(barrier, len(others))
    to_next = pltpu.make_async_remote_copy(
        src_ref=lat.at[pl.ds(t - 16, 16)],
        dst_ref=edge,
        send_sem=esem.at[0],
        recv_sem=esem.at[1],
        device_id={"tm": jnp.minimum(mt + 1, n_tm - 1)},
        device_id_type=MESH,
    )

    @pl.when(mt < n_tm - 1)
    def _():
        to_next.start()

    parts = (
        (1, pl.ds(1, t // PAGE - 1)),
        (0, pl.ds(1, t // PAGE - 1)),
        (slice(None), pl.ds(0, 1)),
    )

    def away(k, i):
        target = peer(me, k, n_reg)
        half, rows = parts[i]
        return pltpu.make_async_remote_copy(
            src_ref=send.at[head_of(target, n_reg, mt)[0], half, rows],
            dst_ref=out_ref.at[half, me, rows],
            send_sem=ssem.at[i, k],
            recv_sem=rsem.at[i, me],
            device_id={"region": target},
            device_id_type=MESH,
        )

    def each(act):
        for k in range(1, n_reg):

            @pl.when(head_of(peer(me, k, n_reg), n_reg, mt)[1])
            def _():
                act(k)

    def tell(j):
        return pltpu.make_async_remote_copy(
            src_ref=csend,
            dst_ref=cbuf.at[mt, me],
            send_sem=tsem.at[0, j],
            recv_sem=tsem.at[1, mt * n_reg + me],
            device_id=place(*others[j]),
            device_id_type=MESH,
        )

    for j in range(len(others)):
        tell(j).start()
    each(lambda k: away(k, 0).start())
    loads[4].wait()
    put(dot(hidden, wbuf[2]).astype(bf16), t, 0, 0)
    loads[5].wait()
    put(dot(hidden, wbuf[3]).astype(bf16), t, 0, hd)
    each(lambda k: away(k, 1).start())

    @pl.when(mt > 0)
    def _():
        to_next.wait_recv()
        ext[0:8, :] = edge[8:16, :].astype(f32)
        top = hide(16)
        put(dot(top, wbuf[1]).astype(bf16), 16, 1, 0)
        put(dot(top, wbuf[2]).astype(bf16), 16, 0, 0)
        put(dot(top, wbuf[3]).astype(bf16), 16, 0, hd)

    each(lambda k: away(k, 2).start())
    here = pltpu.make_async_copy(send.at[head], out_ref.at[:, me], lsem.at[0])

    @pl.when(is_head)
    def _():
        here.start()

    for j in range(len(others)):
        k, c = others[j]
        where = place(k, c)
        slot = where["tm"] * n_reg + where["region"]
        pltpu.make_async_copy(csend, cbuf.at[where["tm"], where["region"]], tsem.at[1, slot]).wait()
    pages = t // PAGE
    zero = jnp.zeros(csend.shape, i32)
    slot = lax.broadcasted_iota(i32, csend.shape, 1)

    def used(c, r):
        return (cbuf[c, r] + (PAGE - 1)) // PAGE

    most = zero
    for c in range(n_tm):
        total = zero
        for r in range(n_reg):
            total = total + used(c, r)
        most = jnp.maximum(most, total)
    pick = zero
    for cap in caps[:-1]:
        pick = pick + jnp.where(most * PAGE > cap, 1, 0)
    pick_ref[0, 0] = jnp.max(pick.astype(f32)).astype(i32)
    end, source, rows_left, begin = zero, zero, zero, zero
    for r in range(n_reg):
        n = used(mt, r)
        mine = jnp.logical_and(slot >= end, slot < end + n)
        source = jnp.where(mine, slot - end + r * pages, source)
        rows_left = jnp.where(mine, cbuf[mt, r] - (slot - end) * PAGE, rows_left)
        begin = jnp.where(slot == r, end, begin)
        end = end + n
    counts = zero
    for r in range(n_reg):
        counts = jnp.where(slot == r, cbuf[mt, r], counts)
    for i, row in enumerate((source, rows_left, begin, counts)):
        table_ref[i : i + 1, :] = row

    def done(k):
        for i in range(3):
            away(k, i).wait_send()

    each(done)
    for j in range(len(others)):
        tell(j).wait_send()

    @pl.when(mt < n_tm - 1)
    def _():
        to_next.wait_send()

    @pl.when(is_head)
    def _():
        here.wait()
        for k in range(1, n_reg):
            s = peer(me, k, n_reg)
            for i, (half, rows) in enumerate(parts):
                there = out_ref.at[half, s, rows]
                pltpu.make_async_copy(send.at[0, half, rows], there, rsem.at[i, s]).wait()


def work_kernel(
    n_reg, n_tm, cap, chunk_ref, tbl_ref, ck_ref, wq_ref, wk_ref, wv_ref,
    out_ref,
    chunk, qk, ka, vg, kt, qt, gt, qg, sbuf, wbuf, dkv, dqp, part,
    got, wts, xs, ext, wsem, esem, ssem, rsem, lsem,
):
    me = lax.axis_index("region")
    mt = lax.axis_index("tm")
    t, d = out_ref.shape[1], out_ref.shape[2]
    hd = d // H
    width = 2 * hd
    inv_root = 1.0 / math.sqrt(hd)
    blocks = cap // BLK
    subs = blocks if blocks <= 5 else 4
    supers = blocks // subs
    step = BLK // PAGE
    barrier = pltpu.get_barrier_semaphore()
    head, is_head = head_of(me, n_reg, mt)

    def each(act):
        for k in range(1, n_reg):
            r = peer(me, k, n_reg)

            @pl.when(head_of(r, n_reg, mt)[1])
            def _():
                act(r)

    each(
        lambda r: pl.semaphore_signal(
            barrier, inc=1, device_id={"region": r}, device_id_type=MESH
        )
    )

    @pl.when(mt < n_tm - 1)
    def _():
        up = {"tm": jnp.minimum(mt + 1, n_tm - 1)}
        pl.semaphore_signal(barrier, inc=1, device_id=up, device_id_type=MESH)

    fetch = pltpu.make_async_copy(chunk_ref, chunk, lsem.at[1])

    @pl.when(is_head)
    def _():
        fetch.start()

    loads = [
        pltpu.make_async_copy(ref, wts.at[i], wsem.at[i])
        for i, ref in enumerate((wq_ref, wk_ref, wv_ref))
    ]
    for load in loads:
        load.start()
    peers = jnp.where(is_head, n_reg - 1, 0) + jnp.minimum(mt, 1)

    def lane(rows):
        return lax.broadcasted_iota(i32, (rows, width), 1)

    def away(r, k):
        return pltpu.make_async_remote_copy(
            src_ref=part.at[r],
            dst_ref=got.at[head],
            send_sem=ssem.at[k],
            recv_sem=rsem.at[head],
            device_id={"region": r},
            device_id_type=MESH,
        )

    here = pltpu.make_async_copy(part.at[me], got.at[head], lsem.at[0])

    @pl.when(is_head)
    def _():
        fetch.wait()

        def pack(p, c):
            source = tbl_ref[0, p]
            rows = tbl_ref[1, p]
            a = chunk[0, source]
            b = chunk[1, source]
            dead = lax.broadcasted_iota(i32, (PAGE, width), 0) >= rows
            bias = jnp.where(jnp.logical_and(lane(PAGE) == 0, dead), NEG, 0.0)
            to = pl.ds(pl.multiple_of(p * PAGE, PAGE), PAGE)
            qk[to, :] = a
            ka[to, :] = jnp.where(lane(PAGE) < hd, bias, a.astype(f32)).astype(bf16)
            vg[to, :] = jnp.where(dead, 0.0, b.astype(f32)).astype(bf16)
            return c

        lax.fori_loop(0, cap // PAGE, pack, 0, unroll=4)

        def ready(i, c):
            at = pl.multiple_of(i * BLK, BLK)
            a = qk[pl.ds(at, BLK), :]
            b = vg[pl.ds(at, BLK), :]
            a_t = a.T
            scaled = (a_t[0:hd, :].astype(f32) * inv_root).astype(bf16)
            one = jnp.where(lax.broadcasted_iota(i32, (hd, BLK), 0) == 0, 1.0, 0.0)
            qt[i] = jnp.concatenate([one.astype(bf16), scaled], axis=0)
            kt[i] = a_t[hd:, :]
            gt[i] = jnp.concatenate([b.T[hd:, :], jnp.zeros((hd, BLK), bf16)], axis=0)
            low = lane(BLK) < hd
            qg[i, 0:BLK, :] = jnp.where(low, a.astype(f32) * inv_root, 0.0).astype(bf16)
            qg[i, BLK:, :] = jnp.where(low, 0.0, b.astype(f32)).astype(bf16)
            dkv[pl.ds(i * step, step)] = jnp.zeros((step, PAGE, width), f32)
            return c

        lax.fori_loop(0, blocks, ready, 0)

        def fold(x, op):
            return op(x.reshape(BLK // 8, 8, BLK), axis=0)

        def per_queries(qi, c):
            qat, gat = qt[qi], gt[qi]

            def first(ki, m):
                for u in range(subs):
                    kat = pl.multiple_of((ki * subs + u) * BLK, BLK)
                    s = dot(ka[pl.ds(kat, BLK), :], qat)
                    wbuf[ki * subs + u] = dot(vg[pl.ds(kat, BLK), :], gat)
                    sbuf[ki * subs + u] = s
                    m = jnp.maximum(m, fold(s, jnp.max))
                return m

            m = lax.fori_loop(0, supers, first, jnp.full((8, BLK), NEG, f32))
            m = jnp.max(m, axis=0, keepdims=True)

            def middle(ki, carry):
                l, dl = carry
                for u in range(subs):
                    p = jnp.exp(sbuf[ki * subs + u] - m)
                    sbuf[ki * subs + u] = p
                    l = l + fold(p, jnp.sum)
                    dl = dl + fold(p * wbuf[ki * subs + u], jnp.sum)
                return l, dl

            none = jnp.zeros((8, BLK), f32)
            l, dl = lax.fori_loop(0, supers, middle, (none, none))
            inv_l = 1.0 / jnp.sum(l, axis=0, keepdims=True)
            delta = jnp.sum(dl, axis=0, keepdims=True) * inv_l
            both = qg[qi]

            def last(ki, dq):
                for u in range(subs):
                    att = sbuf[ki * subs + u] * inv_l
                    ds = (att * (wbuf[ki * subs + u] - delta)).astype(bf16)
                    pair = jnp.concatenate([ds, att.astype(bf16)], axis=1)
                    to = pl.ds((ki * subs + u) * step, step)
                    dkv[to] += dot(pair, both).reshape(step, PAGE, width)
                    dq = dq + dot(kt[ki * subs + u], ds)
                return dq

            dq = lax.fori_loop(0, supers, last, jnp.zeros((hd, BLK), f32))
            dq = jnp.concatenate([dq * inv_root, jnp.zeros((hd, BLK), f32)], axis=0)
            dqp[pl.ds(qi * step, step)] = dq.T.reshape(step, PAGE, width)
            return c

        lax.fori_loop(0, blocks, per_queries, 0)

    @pl.when(peers > 0)
    def _():
        pl.semaphore_wait(barrier, peers)

    @pl.when(is_head)
    def _():
        for k in list(range(1, n_reg)) + [0]:
            r = peer(me, k, n_reg)
            begin = tbl_ref[2, r]
            live = lax.broadcasted_iota(i32, (t, width), 0) < tbl_ref[3, r]

            def rows_of(ref):
                pages = [ref[begin + j] for j in range(t // PAGE)]
                return jnp.where(live, jnp.concatenate(pages, axis=0), 0.0)

            both, dq = rows_of(dkv), rows_of(dqp)
            part[r, 0:t, :] = both.astype(bf16)
            pair = jnp.concatenate([dq[0 : t // 2, 0:hd], dq[t // 2 :, 0:hd]], axis=1)
            part[r, t:, :] = pair.astype(bf16)
            if k:
                away(r, k).start()
            else:
                here.start()
        here.wait()

    for h in range(H):

        @pl.when(owner(h, n_reg, mt) != me)
        def _():
            pltpu.make_async_copy(part.at[0], got.at[h], rsem.at[h]).wait()

    for h in range(H):
        cols = slice(h * hd, (h + 1) * hd)
        xs[0, 0 : t // 2, cols] = got[h, t:, 0:hd]
        xs[0, t // 2 :, cols] = got[h, t:, hd:]
        xs[1, :, cols] = got[h, 0:t, 0:hd]
        xs[2, :, cols] = got[h, 0:t, hd:]
    for load in loads:
        load.wait()
    side = dot_t(xs[1], wts[1]) + dot_t(xs[2], wts[2])
    ext[0:t, :] = dot_t(xs[0], wts[0]) + side

    to_prev = pltpu.make_async_remote_copy(
        src_ref=ext.at[pl.ds(0, 8)],
        dst_ref=ext.at[pl.ds(t, 8)],
        send_sem=esem.at[0],
        recv_sem=esem.at[1],
        device_id={"tm": jnp.maximum(mt - 1, 0)},
        device_id_type=MESH,
    )

    @pl.when(mt > 0)
    def _():
        to_prev.start()

    @pl.when(is_head)
    def _():
        for k in range(1, n_reg):
            away(peer(me, k, n_reg), k).wait_send()

    @pl.when(mt == n_tm - 1)
    def _():
        ext[t : t + 8, :] = jnp.zeros((8, d), f32)

    @pl.when(mt < n_tm - 1)
    def _():
        to_prev.wait_recv()

    total = ck_ref[0:1, :] * ext[0:t, :]
    for j in range(1, KW):
        total = total + ck_ref[j : j + 1, :] * ext[j : j + t, :]
    out_ref[0] = total.astype(bf16)

    @pl.when(mt > 0)
    def _():
        to_prev.wait_send()


def shards(n_reg, n_tm, latents, output_grad, conv_kernel, w_query, w_key, w_value, w_out, live_counts):
    _, t, d = latents.shape
    hd = d // H
    dma = pltpu.SemaphoreType.DMA
    caps = caps_of(n_reg * t)
    lanes = max(128, n_reg * t // PAGE)
    chunks, table, pick = pl.pallas_call(
        functools.partial(spread_kernel, n_reg, n_tm, caps),
        out_shape=(
            jax.ShapeDtypeStruct((2, n_reg, t // PAGE, PAGE, 2 * hd), bf16),
            jax.ShapeDtypeStruct((4, lanes), i32),
            jax.ShapeDtypeStruct((1, 1), i32),
        ),
        in_specs=[ANY, ANY, VM, SM, ANY, ANY, ANY, ANY],
        out_specs=(ANY, VM, SM),
        scratch_shapes=[
            pltpu.VMEM((4, d, d), bf16),
            pltpu.VMEM((t, d), bf16),
            pltpu.VMEM((t, d), bf16),
            pltpu.VMEM((t + 8, d), f32),
            pltpu.VMEM((16, d), bf16),
            pltpu.VMEM((H, 2, t // PAGE, PAGE, 2 * hd), bf16),
            pltpu.VMEM((1, lanes), i32),
            pltpu.VMEM((n_tm, n_reg, 1, lanes), i32),
            dma((6,)),
            dma((2,)),
            dma((3, n_reg)),
            dma((3, n_reg)),
            dma((2, n_reg * n_tm)),
            dma((1,)),
        ],
        compiler_params=pltpu.CompilerParams(collective_id=0, has_side_effects=True),
        name="spread",
    )(latents, output_grad, conv_kernel, live_counts, w_query, w_key, w_value, w_out)

    def work(i, cap):
        blocks = cap // BLK
        return pl.pallas_call(
            functools.partial(work_kernel, n_reg, n_tm, cap),
            out_shape=jax.ShapeDtypeStruct((1, t, d), bf16),
            in_specs=[ANY, SM, VM, ANY, ANY, ANY],
            out_specs=VM,
            scratch_shapes=[
                pltpu.VMEM((2, n_reg * t // PAGE, PAGE, 2 * hd), bf16),
                pltpu.VMEM((cap, 2 * hd), bf16),
                pltpu.VMEM((cap, 2 * hd), bf16),
                pltpu.VMEM((cap, 2 * hd), bf16),
                pltpu.VMEM((blocks, hd, BLK), bf16),
                pltpu.VMEM((blocks, 2 * hd, BLK), bf16),
                pltpu.VMEM((blocks, 2 * hd, BLK), bf16),
                pltpu.VMEM((blocks, 2 * BLK, 2 * hd), bf16),
                pltpu.VMEM((blocks, BLK, BLK), f32),
                pltpu.VMEM((blocks, BLK, BLK), f32),
                pltpu.VMEM(((cap + t) // PAGE, PAGE, 2 * hd), f32),
                pltpu.VMEM(((cap + t) // PAGE, PAGE, 2 * hd), f32),
                pltpu.VMEM((n_reg, t + t // 2, 2 * hd), bf16),
                pltpu.VMEM((H, t + t // 2, 2 * hd), bf16),
                pltpu.VMEM((3, d, d), bf16),
                pltpu.VMEM((3, t, d), bf16),
                pltpu.VMEM((t + 8, d), f32),
                dma((3,)),
                dma((2,)),
                dma((n_reg,)),
                dma((H,)),
                dma((2,)),
            ],
            compiler_params=pltpu.CompilerParams(collective_id=i + 1, has_side_effects=True),
            name=f"work{cap}",
        )

    return lax.switch(
        pick[0, 0],
        [work(i, cap) for i, cap in enumerate(caps)],
        chunks.reshape(2, n_reg * t // PAGE, PAGE, 2 * hd), table, conv_kernel, w_query, w_key, w_value,
    )


def solution(mesh):
    shard = P("region", "tm", None)
    in_specs = (shard, shard, P(), P(), P(), P(), P(), P("region", "tm"))
    body = functools.partial(shards, mesh.shape["region"], mesh.shape["tm"])
    return jax.shard_map(body, mesh=mesh, in_specs=in_specs, out_specs=shard, check_vma=False)
```

```python
import functools
import math

import jax
import jax.numpy as jnp
from jax import lax
from jax.experimental import pallas as pl
from jax.experimental.pallas import tpu as pltpu
from jax.sharding import PartitionSpec as P

H = 12
KW = 4
BLK = 256
PAGE = 16
CAPS = (1024, 1280)
GROUP = 4
SPREAD_VMEM = 20 << 20
WORK_VMEM = 40 << 20
FINISH_VMEM = 8 << 20
NEG = -1e30
bf16 = jnp.bfloat16
f32 = jnp.float32
i32 = jnp.int32
VM = pl.BlockSpec(memory_space=pltpu.VMEM)
SM = pl.BlockSpec(memory_space=pltpu.SMEM)
ANY = pl.BlockSpec(memory_space=pl.ANY)
HBM = pl.BlockSpec(memory_space=pltpu.MemorySpace.HBM)
MESH = pl.DeviceIdType.MESH


def dot(a, b):
    return jnp.dot(a, b, preferred_element_type=f32)


def dot_t(a, b):
    return lax.dot_general(a, b, (((1,), (1,)), ((), ())), preferred_element_type=f32)


def owner(h, n_reg, mt):
    base = (h * n_reg) // H
    if n_reg % 4:
        return base
    return base // 4 * 4 + (base + base // 4 + 2 * mt) % 4


def head_of(me, n_reg, mt):
    base = me
    if n_reg % 4 == 0:
        base = me // 4 * 4 + (me + 3 * (me // 4) + 2 * mt) % 4
    h = (base * H + n_reg - 1) // n_reg
    return jnp.minimum(h, H - 1), jnp.logical_and(h < H, (h * n_reg) // H == base)


def peer(me, step, n):
    return lax.rem(me + step, n)


def far(x):
    return pltpu.with_memory_space_constraint(x, pltpu.MemorySpace.HBM)


def caps_of(n):
    return [c for c in CAPS if c < n] + [-(-n // 1024) * 1024]


def spread_kernel(
    n_reg, n_tm, caps, lat_ref, og_ref, taps_ref, cnt_ref, wq_ref, wk_ref, wv_ref, wo_ref,
    out_ref, table_ref, pick_ref,
    ck_ref, wbuf, lat, og, ext, edge, send, csend, cbuf, wsem, esem, ssem, rsem, tsem, lsem,
):
    me = lax.axis_index("region")
    mt = lax.axis_index("tm")
    t, d = lat_ref.shape[1], lat_ref.shape[2]
    hd = d // H
    barrier = pltpu.get_barrier_semaphore()
    others = [
        (k, c) for k in range(n_reg) for c in range(n_tm) if (k, c) != (0, 0)
    ]

    def place(k, c):
        return {"region": peer(me, k, n_reg), "tm": lax.rem(mt + c, n_tm)}

    for k, c in others:
        pl.semaphore_signal(barrier, inc=1, device_id=place(k, c), device_id_type=MESH)
    loads = [
        pltpu.make_async_copy(ref, dst, wsem.at[i])
        for i, (ref, dst) in enumerate(
            (
                (lat_ref.at[0], lat),
                (og_ref.at[0], og),
                (wo_ref, wbuf.at[0]),
                (wv_ref, wbuf.at[1]),
                (wq_ref, wbuf.at[2]),
                (wk_ref, wbuf.at[3]),
                (taps_ref, ck_ref),
            )
        )
    ]
    for load in loads:
        load.start()
    head, is_head = head_of(me, n_reg, mt)

    count = cnt_ref[0, 0]
    csend[...] = jnp.zeros(csend.shape, i32) + count
    cbuf[mt, me] = jnp.zeros(csend.shape, i32) + count

    def hide(rows):
        hidden = ck_ref[0:1, :] * ext[8 : 8 + rows, :]
        for j in range(1, KW):
            hidden = hidden + ck_ref[j : j + 1, :] * ext[8 - j : 8 - j + rows, :]
        return hidden.astype(bf16)

    def put(x, rows, half, first):
        for h in range(H):
            part = x[:, h * hd : (h + 1) * hd].reshape(rows // PAGE, PAGE, hd)
            send[h, half, 0 : rows // PAGE, :, first : first + hd] = part

    loads[0].wait()
    loads[6].wait()
    ext[0:8, :] = jnp.zeros((8, d), f32)
    ext[8 : 8 + t, :] = lat[...].astype(f32)
    hidden = hide(t)
    loads[1].wait()
    loads[2].wait()
    live = lax.broadcasted_iota(i32, (t, 1), 0) < count
    g = jnp.where(live, dot_t(og[...], wbuf[0]), 0.0).astype(bf16)
    put(g, t, 1, hd)
    loads[3].wait()
    put(dot(hidden, wbuf[1]).astype(bf16), t, 1, 0)

    pl.semaphore_wait(barrier, len(others))
    to_next = pltpu.make_async_remote_copy(
        src_ref=lat.at[pl.ds(t - 16, 16)],
        dst_ref=edge,
        send_sem=esem.at[0],
        recv_sem=esem.at[1],
        device_id={"tm": jnp.minimum(mt + 1, n_tm - 1)},
        device_id_type=MESH,
    )

    @pl.when(mt < n_tm - 1)
    def _():
        to_next.start()

    parts = (
        (1, pl.ds(1, t // PAGE - 1)),
        (0, pl.ds(1, t // PAGE - 1)),
        (slice(None), pl.ds(0, 1)),
    )

    def away(k, i):
        target = peer(me, k, n_reg)
        half, rows = parts[i]
        return pltpu.make_async_remote_copy(
            src_ref=send.at[head_of(target, n_reg, mt)[0], half, rows],
            dst_ref=out_ref.at[half, me, rows],
            send_sem=ssem.at[i, k],
            recv_sem=rsem.at[i, me],
            device_id={"region": target},
            device_id_type=MESH,
        )

    def each(act):
        for k in range(1, n_reg):

            @pl.when(head_of(peer(me, k, n_reg), n_reg, mt)[1])
            def _():
                act(k)

    def tell(j):
        return pltpu.make_async_remote_copy(
            src_ref=csend,
            dst_ref=cbuf.at[mt, me],
            send_sem=tsem.at[0, j],
            recv_sem=tsem.at[1, mt * n_reg + me],
            device_id=place(*others[j]),
            device_id_type=MESH,
        )

    for j in range(len(others)):
        tell(j).start()
    each(lambda k: away(k, 0).start())
    loads[4].wait()
    put(dot(hidden, wbuf[2]).astype(bf16), t, 0, 0)
    loads[5].wait()
    put(dot(hidden, wbuf[3]).astype(bf16), t, 0, hd)
    each(lambda k: away(k, 1).start())

    @pl.when(mt > 0)
    def _():
        to_next.wait_recv()
        ext[0:8, :] = edge[8:16, :].astype(f32)
        top = hide(16)
        put(dot(top, wbuf[1]).astype(bf16), 16, 1, 0)
        put(dot(top, wbuf[2]).astype(bf16), 16, 0, 0)
        put(dot(top, wbuf[3]).astype(bf16), 16, 0, hd)

    each(lambda k: away(k, 2).start())
    here = pltpu.make_async_copy(send.at[head], out_ref.at[:, me], lsem.at[0])

    @pl.when(is_head)
    def _():
        here.start()

    for j in range(len(others)):
        k, c = others[j]
        where = place(k, c)
        slot = where["tm"] * n_reg + where["region"]
        pltpu.make_async_copy(csend, cbuf.at[where["tm"], where["region"]], tsem.at[1, slot]).wait()
    pages = t // PAGE
    zero = jnp.zeros(csend.shape, i32)
    slot = lax.broadcasted_iota(i32, csend.shape, 1)

    def used(c, r):
        return (cbuf[c, r] + (PAGE - 1)) // PAGE

    most = zero
    for c in range(n_tm):
        total = zero
        for r in range(n_reg):
            total = total + used(c, r)
        most = jnp.maximum(most, total)
    pick = zero
    for cap in caps[:-1]:
        pick = pick + jnp.where(most * PAGE > cap, 1, 0)
    pick_ref[0, 0] = jnp.max(pick.astype(f32)).astype(i32)
    end, source, rows_left, begin = zero, zero, zero, zero
    for r in range(n_reg):
        n = used(mt, r)
        mine = jnp.logical_and(slot >= end, slot < end + n)
        source = jnp.where(mine, slot - end + r * pages, source)
        rows_left = jnp.where(mine, cbuf[mt, r] - (slot - end) * PAGE, rows_left)
        begin = jnp.where(slot == r, end, begin)
        end = end + n
    counts = zero
    for r in range(n_reg):
        counts = jnp.where(slot == r, cbuf[mt, r], counts)
    for i, row in enumerate((source, rows_left, begin, counts)):
        table_ref[i : i + 1, :] = row

    def done(k):
        for i in range(3):
            away(k, i).wait_send()

    each(done)
    for j in range(len(others)):
        tell(j).wait_send()

    @pl.when(mt < n_tm - 1)
    def _():
        to_next.wait_send()

    @pl.when(is_head)
    def _():
        here.wait()
        for k in range(1, n_reg):
            s = peer(me, k, n_reg)
            for i, (half, rows) in enumerate(parts):
                there = out_ref.at[half, s, rows]
                pltpu.make_async_copy(send.at[0, half, rows], there, rsem.at[i, s]).wait()


def work_kernel(
    n_reg, n_tm, cap, chunk, tbl_ref, wq_ref, wk_ref, wv_ref,
    ext_ref,
    qk, ka, vg, kt, qt, gt, qg, sbuf, wbuf, dkv, dqp, part,
    got, xs, esem, ssem, rsem, lsem,
):
    me = lax.axis_index("region")
    mt = lax.axis_index("tm")
    t, d = ext_ref.shape[0] - 8, ext_ref.shape[1]
    hd = d // H
    width = 2 * hd
    inv_root = 1.0 / math.sqrt(hd)
    blocks = cap // BLK
    subs = blocks if blocks <= 5 else 4
    supers = blocks // subs
    step = BLK // PAGE
    barrier = pltpu.get_barrier_semaphore()
    head, is_head = head_of(me, n_reg, mt)

    def each(act):
        for k in range(1, n_reg):
            r = peer(me, k, n_reg)

            @pl.when(head_of(r, n_reg, mt)[1])
            def _():
                act(r)

    each(
        lambda r: pl.semaphore_signal(
            barrier, inc=1, device_id={"region": r}, device_id_type=MESH
        )
    )

    @pl.when(mt < n_tm - 1)
    def _():
        up = {"tm": jnp.minimum(mt + 1, n_tm - 1)}
        pl.semaphore_signal(barrier, inc=1, device_id=up, device_id_type=MESH)

    peers = jnp.where(is_head, n_reg - 1, 0) + jnp.minimum(mt, 1)

    def lane(rows):
        return lax.broadcasted_iota(i32, (rows, width), 1)

    def away(r, k):
        return pltpu.make_async_remote_copy(
            src_ref=part.at[r],
            dst_ref=got.at[head],
            send_sem=ssem.at[k],
            recv_sem=rsem.at[head],
            device_id={"region": r},
            device_id_type=MESH,
        )

    here = pltpu.make_async_copy(part.at[me], got.at[head], lsem.at[0])

    @pl.when(is_head)
    def _():
        def pack(p, c):
            source = tbl_ref[0, p]
            rows = tbl_ref[1, p]
            a = chunk[0, source]
            b = chunk[1, source]
            dead = lax.broadcasted_iota(i32, (PAGE, width), 0) >= rows
            bias = jnp.where(jnp.logical_and(lane(PAGE) == 0, dead), NEG, 0.0)
            to = pl.ds(pl.multiple_of(p * PAGE, PAGE), PAGE)
            qk[to, :] = a
            ka[to, :] = jnp.where(lane(PAGE) < hd, bias, a.astype(f32)).astype(bf16)
            vg[to, :] = jnp.where(dead, 0.0, b.astype(f32)).astype(bf16)
            return c

        lax.fori_loop(0, cap // PAGE, pack, 0, unroll=4)

        def ready(i, c):
            at = pl.multiple_of(i * BLK, BLK)
            a = qk[pl.ds(at, BLK), :]
            b = vg[pl.ds(at, BLK), :]
            a_t = a.T
            scaled = (a_t[0:hd, :].astype(f32) * inv_root).astype(bf16)
            one = jnp.where(lax.broadcasted_iota(i32, (hd, BLK), 0) == 0, 1.0, 0.0)
            qt[i] = jnp.concatenate([one.astype(bf16), scaled], axis=0)
            kt[i] = a_t[hd:, :]
            gt[i] = jnp.concatenate([b.T[hd:, :], jnp.zeros((hd, BLK), bf16)], axis=0)
            low = lane(BLK) < hd
            qg[i, 0:BLK, :] = jnp.where(low, a.astype(f32) * inv_root, 0.0).astype(bf16)
            qg[i, BLK:, :] = jnp.where(low, 0.0, b.astype(f32)).astype(bf16)
            dkv[pl.ds(i * step, step)] = jnp.zeros((step, PAGE, width), f32)
            return c

        lax.fori_loop(0, blocks, ready, 0)

        def fold(x, op):
            return op(x.reshape(BLK // 8, 8, BLK), axis=0)

        def per_queries(qi, c):
            qat, gat = qt[qi], gt[qi]

            def first(ki, m):
                for u in range(subs):
                    kat = pl.multiple_of((ki * subs + u) * BLK, BLK)
                    s = dot(ka[pl.ds(kat, BLK), :], qat)
                    wbuf[ki * subs + u] = dot(vg[pl.ds(kat, BLK), :], gat)
                    sbuf[ki * subs + u] = s
                    m = jnp.maximum(m, fold(s, jnp.max))
                return m

            m = lax.fori_loop(0, supers, first, jnp.full((8, BLK), NEG, f32))
            m = jnp.max(m, axis=0, keepdims=True)

            def middle(ki, carry):
                l, dl = carry
                for u in range(subs):
                    p = jnp.exp(sbuf[ki * subs + u] - m)
                    sbuf[ki * subs + u] = p
                    l = l + fold(p, jnp.sum)
                    dl = dl + fold(p * wbuf[ki * subs + u], jnp.sum)
                return l, dl

            none = jnp.zeros((8, BLK), f32)
            l, dl = lax.fori_loop(0, supers, middle, (none, none))
            inv_l = 1.0 / jnp.sum(l, axis=0, keepdims=True)
            delta = jnp.sum(dl, axis=0, keepdims=True) * inv_l
            both = qg[qi]

            def last(ki, dq):
                for u in range(subs):
                    att = sbuf[ki * subs + u] * inv_l
                    ds = (att * (wbuf[ki * subs + u] - delta)).astype(bf16)
                    pair = jnp.concatenate([ds, att.astype(bf16)], axis=1)
                    to = pl.ds((ki * subs + u) * step, step)
                    dkv[to] += dot(pair, both).reshape(step, PAGE, width)
                    dq = dq + dot(kt[ki * subs + u], ds)
                return dq

            dq = lax.fori_loop(0, supers, last, jnp.zeros((hd, BLK), f32))
            dq = jnp.concatenate([dq * inv_root, jnp.zeros((hd, BLK), f32)], axis=0)
            dqp[pl.ds(qi * step, step)] = dq.T.reshape(step, PAGE, width)
            return c

        lax.fori_loop(0, blocks, per_queries, 0)

    @pl.when(peers > 0)
    def _():
        pl.semaphore_wait(barrier, peers)

    @pl.when(is_head)
    def _():
        for k in list(range(1, n_reg)) + [0]:
            r = peer(me, k, n_reg)
            begin = tbl_ref[2, r]
            live = lax.broadcasted_iota(i32, (t, width), 0) < tbl_ref[3, r]

            def rows_of(ref):
                pages = [ref[begin + j] for j in range(t // PAGE)]
                return jnp.where(live, jnp.concatenate(pages, axis=0), 0.0)

            both, dq = rows_of(dkv), rows_of(dqp)
            part[r, 0:t, :] = both.astype(bf16)
            pair = jnp.concatenate([dq[0 : t // 2, 0:hd], dq[t // 2 :, 0:hd]], axis=1)
            part[r, t:, :] = pair.astype(bf16)
            if k:
                away(r, k).start()
            else:
                here.start()
        here.wait()

    wide = GROUP * hd
    groups = H // GROUP
    for j in range(groups):
        g = jnp.where(2 * me < n_reg, j, groups - 1 - j)
        for i in range(GROUP):
            h = g * GROUP + i

            @pl.when(owner(h, n_reg, mt) != me)
            def _():
                pltpu.make_async_copy(part.at[0], got.at[h], rsem.at[h]).wait()

            cols = slice(i * hd, (i + 1) * hd)
            xs[0, 0 : t // 2, cols] = got[h, t:, 0:hd]
            xs[0, t // 2 :, cols] = got[h, t:, hd:]
            xs[1, :, cols] = got[h, 0:t, 0:hd]
            xs[2, :, cols] = got[h, 0:t, hd:]
        cols = pl.ds(pl.multiple_of(g * wide, wide), wide)
        add = dot_t(xs[0], wq_ref[:, cols]) + (
            dot_t(xs[1], wk_ref[:, cols]) + dot_t(xs[2], wv_ref[:, cols])
        )
        if j == 0:
            ext_ref[0:t, :] = add
        else:
            ext_ref[0:t, :] += add

    to_prev = pltpu.make_async_remote_copy(
        src_ref=ext_ref.at[pl.ds(0, 8)],
        dst_ref=ext_ref.at[pl.ds(t, 8)],
        send_sem=esem.at[0],
        recv_sem=esem.at[1],
        device_id={"tm": jnp.maximum(mt - 1, 0)},
        device_id_type=MESH,
    )

    @pl.when(mt > 0)
    def _():
        to_prev.start()

    @pl.when(is_head)
    def _():
        for k in range(1, n_reg):
            away(peer(me, k, n_reg), k).wait_send()

    @pl.when(mt == n_tm - 1)
    def _():
        ext_ref[t : t + 8, :] = jnp.zeros((8, d), f32)

    @pl.when(mt < n_tm - 1)
    def _():
        to_prev.wait_recv()

    @pl.when(mt > 0)
    def _():
        to_prev.wait_send()


def finish_kernel(ext_ref, ck_ref, out_ref):
    t = out_ref.shape[1]
    total = ck_ref[0:1, :] * ext_ref[0:t, :]
    for j in range(1, KW):
        total = total + ck_ref[j : j + 1, :] * ext_ref[j : j + t, :]
    out_ref[0] = total.astype(bf16)


def shards(n_reg, n_tm, latents, output_grad, conv_kernel, w_query, w_key, w_value, w_out, live_counts):
    _, t, d = latents.shape
    hd = d // H
    dma = pltpu.SemaphoreType.DMA
    caps = caps_of(n_reg * t)
    lanes = max(128, n_reg * t // PAGE)
    chunks, table, pick = pl.pallas_call(
        functools.partial(spread_kernel, n_reg, n_tm, caps),
        out_shape=(
            jax.ShapeDtypeStruct((2, n_reg, t // PAGE, PAGE, 2 * hd), bf16),
            jax.ShapeDtypeStruct((4, lanes), i32),
            jax.ShapeDtypeStruct((1, 1), i32),
        ),
        in_specs=[HBM, HBM, HBM, SM, HBM, HBM, HBM, HBM],
        out_specs=(ANY, VM, SM),
        scratch_shapes=[
            pltpu.VMEM(conv_kernel.shape, f32),
            pltpu.VMEM((4, d, d), bf16),
            pltpu.VMEM((t, d), bf16),
            pltpu.VMEM((t, d), bf16),
            pltpu.VMEM((t + 8, d), f32),
            pltpu.VMEM((16, d), bf16),
            pltpu.VMEM((H, 2, t // PAGE, PAGE, 2 * hd), bf16),
            pltpu.VMEM((1, lanes), i32),
            pltpu.VMEM((n_tm, n_reg, 1, lanes), i32),
            dma((7,)),
            dma((2,)),
            dma((3, n_reg)),
            dma((3, n_reg)),
            dma((2, n_reg * n_tm)),
            dma((1,)),
        ],
        compiler_params=pltpu.CompilerParams(
            collective_id=0, has_side_effects=True, vmem_limit_bytes=SPREAD_VMEM
        ),
        name="spread",
    )(far(latents), far(output_grad), far(conv_kernel), live_counts, far(w_query), far(w_key), far(w_value), far(w_out))

    def work(i, cap):
        blocks = cap // BLK
        return pl.pallas_call(
            functools.partial(work_kernel, n_reg, n_tm, cap),
            out_shape=jax.ShapeDtypeStruct((t + 8, d), f32),
            in_specs=[VM, SM, VM, VM, VM],
            out_specs=VM,
            scratch_shapes=[
                pltpu.VMEM((cap, 2 * hd), bf16),
                pltpu.VMEM((cap, 2 * hd), bf16),
                pltpu.VMEM((cap, 2 * hd), bf16),
                pltpu.VMEM((blocks, hd, BLK), bf16),
                pltpu.VMEM((blocks, 2 * hd, BLK), bf16),
                pltpu.VMEM((blocks, 2 * hd, BLK), bf16),
                pltpu.VMEM((blocks, 2 * BLK, 2 * hd), bf16),
                pltpu.VMEM((blocks, BLK, BLK), f32),
                pltpu.VMEM((blocks, BLK, BLK), f32),
                pltpu.VMEM(((cap + t) // PAGE, PAGE, 2 * hd), f32),
                pltpu.VMEM(((cap + t) // PAGE, PAGE, 2 * hd), f32),
                pltpu.VMEM((n_reg, t + t // 2, 2 * hd), bf16),
                pltpu.VMEM((H, t + t // 2, 2 * hd), bf16),
                pltpu.VMEM((3, t, GROUP * hd), bf16),
                dma((2,)),
                dma((n_reg,)),
                dma((H,)),
                dma((1,)),
            ],
            compiler_params=pltpu.CompilerParams(
                collective_id=i + 1, has_side_effects=True, vmem_limit_bytes=WORK_VMEM
            ),
            name=f"work{cap}",
        )

    ext = lax.switch(
        pick[0, 0],
        [work(i, cap) for i, cap in enumerate(caps)],
        chunks.reshape(2, n_reg * t // PAGE, PAGE, 2 * hd), table, w_query, w_key, w_value,
    )
    return pl.pallas_call(
        finish_kernel,
        out_shape=jax.ShapeDtypeStruct((1, t, d), bf16),
        in_specs=[VM, VM],
        out_specs=VM,
        compiler_params=pltpu.CompilerParams(vmem_limit_bytes=FINISH_VMEM),
        name="finish",
    )(ext, conv_kernel)


def solution(mesh):
    shard = P("region", "tm", None)
    in_specs = (shard, shard, P(), P(), P(), P(), P(), P("region", "tm"))
    body = functools.partial(shards, mesh.shape["region"], mesh.shape["tm"])
    return jax.shard_map(body, mesh=mesh, in_specs=in_specs, out_specs=shard, check_vma=False)
```
